32 devices in a mesh: gx: 4 (over y, core), gy: 4 (over z), gz: 2 (over x).
Axes of the slice: x: 2, y: 2, z: 4, core: 2. Of those that a mesh axis runs over, the one named last changes fastest.
Arguments:
- stiffness: float32 [32, 48, 256], P('gx', 'gy', 'gz'), may hold values from 0.5 to 5
- density: float32 [32, 48, 256], P('gx', 'gy', 'gz'), may hold values from 1 to 4
- load: float32 [3, 32, 48, 256], P(None, 'gx', 'gy', 'gz'), may hold values from -6 to 6
- alive: int32 [4, 32, 48, 256], P(None, 'gx', 'gy', 'gz'), may hold values 0 or 1
- surf_coords: float32 [512, 3, 128], P(('gx', 'gy', 'gz')), may hold values from 0 to 1
- surf_nodes: int32 [512, 128], P(('gx', 'gy', 'gz')), may hold values from 0 to 12287
- routes: int32 [4, 512], P(None, ('gx', 'gy', 'gz')), may hold values from 0 to 1, as said below
- pairs: int32 [4, 32, 64, 2], P(None, ('gx', 'gy', 'gz')), may hold values from 0 to 15, as said below
Outputs:
- element_velocity: float32 [3, 32, 48, 256], P(None, 'gx', 'gy', 'gz')
- element_stress: float32 [6, 32, 48, 256], P(None, 'gx', 'gy', 'gz')
The draws below stay inside these ranges and needn't reach their ends.
Inputs may be any that keep to these rules, and one draw needn't show every extreme that they name: `routes`: in every step a device sends at most 8 of its blocks to one box, and all devices of a gz column send exactly 8 blocks to one common box of that column. `pairs`: every slot named is live at that box and step whenever the box holds a block at all.
All inputs are finite; a program needn't handle non-finite values. No bound on the sum of `alive` on one device may be relied on, other than what follows from the above.
Results may differ from the reference program's by a relative error of at most 0.0003.
Values sent between devices are 32-bit elements; how exact they have to be, the bound alone decides.
A program may use at most 64 MiB of HBM per device.

```python
import math
import jax
import jax.numpy as jnp
from jax import lax

CX = 8
CY = 12
CZ = 128
SB = 16
NPAIR = 64
BNODES = 128
STEPS = 4
NX = 32
NY = 48
NZ = 256
BLOCKS = 512
N_GX = 4
N_GY = 4
N_GZ = 2


def contact_plan(key):
    devices = N_GX * N_GY * N_GZ
    columns = N_GX * N_GY
    capacity = max(SB // 4, SB // N_GZ)
    entries = N_GZ * capacity
    key_target = jax.random.fold_in(key, 101)
    key_noise = jax.random.fold_in(key, 202)
    key_shuffle = jax.random.fold_in(key, 303)
    key_picks = jax.random.fold_in(key, 404)
    target = jax.random.randint(key_target, (STEPS, columns), 0, N_GZ)
    target_device = jnp.repeat(target, N_GZ, axis=1)
    entry = jnp.arange(entries, dtype=jnp.int32)
    entry_box = entry // capacity
    noise = jax.random.randint(key_noise, (STEPS, devices, entries), 0, 65536)
    score = jnp.where(entry_box[None, None, :] == target_device[:, :, None], 0, 1 + noise) * entries + entry
    order = jnp.argsort(score, axis=-1)
    chosen = entry_box[order[..., :SB]]
    shuffle = jax.random.randint(key_shuffle, (STEPS, devices, SB), 0, 65536) * SB + jnp.arange(SB, dtype=jnp.int32)
    placing = jnp.argsort(shuffle, axis=-1)
    route_table = jnp.take_along_axis(chosen, placing, axis=-1)
    counts = jnp.sum((route_table[..., None] == jnp.arange(N_GZ, dtype=jnp.int32)).astype(jnp.int32), axis=2)
    counts = counts.reshape(STEPS, columns, N_GZ, N_GZ).transpose(0, 1, 3, 2).reshape(STEPS, devices, N_GZ)
    live = jnp.arange(capacity, dtype=jnp.int32)[None, None, None, :] < counts[..., None]
    live = live.reshape(STEPS, devices, entries)
    live_first = jnp.argsort(jnp.where(live, 0, 1) * entries + entry, axis=-1)
    how_many = jnp.maximum(jnp.sum(live.astype(jnp.int32), axis=-1), 1)
    picks = jax.random.randint(key_picks, (STEPS, devices, NPAIR * 2), 0, 65536) % how_many[..., None]
    slot_table = jnp.take_along_axis(live_first, picks, axis=-1).reshape(STEPS, devices, NPAIR, 2)
    return (route_table.reshape(STEPS, devices * SB).astype(jnp.int32), slot_table.astype(jnp.int32))


def draw_routes(key, part):
    return contact_plan(key)[0]


def draw_pairs(key, part):
    return contact_plan(key)[1]


def plant(values, own_key, smallest, top_value):
    place = [jax.random.randint(jax.random.fold_in(own_key, axis), (), 0, length) for axis, length in enumerate(values.shape)]
    widest = values.shape.index(max(values.shape))
    next_to = place[:widest] + [(place[widest] + 1) % values.shape[widest]] + place[widest + 1:]
    return values.at[tuple(place)].set(smallest).at[tuple(next_to)].set(top_value)


def shard_levels(stream_key, dims, split, least, top_value):
    def one(axis_at, blocks):
        draws = jax.random.uniform(jax.random.fold_in(jax.random.fold_in(stream_key, 6), axis_at), (blocks,), jnp.float32, least / len(split), top_value / len(split))
        return jnp.repeat(jnp.exp(draws), dims[axis_at] // blocks).reshape((-1,) + (1,) * (len(dims) - axis_at - 1))

    loudness = one(*split[0])
    for cut in split[1:]:
        loudness = loudness * one(*cut)
    return loudness


def scatter_about(stream_key, extent, spread, bound, cuts=(), kind=jnp.bfloat16):
    array = spread * jax.random.normal(stream_key, extent, jnp.float32)
    if cuts:
        array = array * shard_levels(stream_key, extent, cuts, -0.22, 0.18)
    return jnp.clip(array, -bound, bound).astype(kind)


def setup_inputs(seed: int = 0) -> dict:
    key_of = jax.random.split(jax.random.key(seed), 9)
    stiffness = jnp.clip(jnp.exp(math.log(5.0) - 2.3025851 * jax.random.uniform(key_of[0], (NX, NY, NZ), jnp.float32) ** shard_levels(key_of[0], (NX, NY, NZ), ((0, 4), (1, 4), (2, 2)), -0.2, 0.2)), 0.5, 5.0)
    density = jnp.clip(jnp.exp(math.log(4.0) - 1.3862944 * jax.random.uniform(key_of[1], (NX, NY, NZ), jnp.float32) ** shard_levels(key_of[1], (NX, NY, NZ), ((0, 4), (1, 4), (2, 2)), -0.2, 0.2)), 1.0, 4.0)
    load = scatter_about(key_of[2], (3, NX, NY, NZ), 1.0, 6.0, ((1, 4), (2, 4), (3, 2)), jnp.float32)
    alive = plant((jax.random.randint(key_of[3], (STEPS, NX, NY, NZ), 0, 10) < 9).astype(jnp.int32), jax.random.fold_in(key_of[3], 1), 0, 1)
    surf_coords = jnp.clip(1.0 * jax.random.uniform(key_of[4], (BLOCKS, 3, BNODES), jnp.float32) ** shard_levels(key_of[4], (BLOCKS, 3, BNODES), ((0, 32),), -0.2, 0.2), 0.0, 1.0)
    surf_nodes = plant(jax.random.randint(key_of[5], (BLOCKS, BNODES), 0, CX * CY * CZ), jax.random.fold_in(key_of[5], 1), 0, (CX * CY * CZ) - 1).astype(jnp.int32)
    routes = draw_routes(jax.random.fold_in(key_of[8], 71), 0)
    pairs = draw_pairs(jax.random.fold_in(key_of[8], 71), 0)
    return dict(stiffness=stiffness, density=density, load=load, alive=alive, surf_coords=surf_coords, surf_nodes=surf_nodes, routes=routes, pairs=pairs)


REPULSION = 1.0
KERNEL_SCALE = 0.08
TIME_STEP = 0.2
HIGHEST = lax.Precision.HIGHEST
CORNERS = [(0, 0, 0), (0, 0, 1), (0, 1, 0), (0, 1, 1), (1, 0, 0), (1, 0, 1), (1, 1, 0), (1, 1, 1)]


def corner(field, offsets):
    size_x = field.shape[1] - 1
    size_y = field.shape[2] - 1
    size_z = field.shape[3] - 1
    return field[:, offsets[0]:offsets[0] + size_x, offsets[1]:offsets[1] + size_y, offsets[2]:offsets[2] + size_z]


def element_stress(disp, modulus):
    grads = []
    for axis in range(3):
        parts = []
        for first in (0, 1):
            for second in (0, 1):
                upper = [first, second]
                upper.insert(axis, 1)
                lower = [first, second]
                lower.insert(axis, 0)
                parts.append(corner(disp, upper) - corner(disp, lower))
        grads.append(0.25 * (parts[0] + parts[1] + parts[2] + parts[3]))
    strain_xx = grads[0][0]
    strain_yy = grads[1][1]
    strain_zz = grads[2][2]
    strain_xy = 0.5 * (grads[1][0] + grads[0][1])
    strain_yz = 0.5 * (grads[2][1] + grads[1][2])
    strain_zx = 0.5 * (grads[0][2] + grads[2][0])
    trace = strain_xx + strain_yy + strain_zz
    return jnp.stack([modulus * (2.0 * strain_xx + trace), modulus * (2.0 * strain_yy + trace),
                      modulus * (2.0 * strain_zz + trace), modulus * 2.0 * strain_xy,
                      modulus * 2.0 * strain_yz, modulus * 2.0 * strain_zx])


def node_forces(stress, load):
    rows = ((stress[0], stress[3], stress[5]), (stress[3], stress[1], stress[4]), (stress[5], stress[4], stress[2]))
    total = jnp.float32(0.0)
    for offsets in CORNERS:
        signs = [2.0 * offsets[0] - 1.0, 2.0 * offsets[1] - 1.0, 2.0 * offsets[2] - 1.0]
        pieces = []
        for index in range(3):
            row = rows[index]
            pieces.append(-0.25 * (signs[0] * row[0] + signs[1] * row[1] + signs[2] * row[2]) + 0.125 * load[index])
        term = jnp.stack(pieces)
        total = total + jnp.pad(term, ((0, 0), (offsets[0], 1 - offsets[0]), (offsets[1], 1 - offsets[1]), (offsets[2], 1 - offsets[2])))
    return total


def node_mass(density):
    share = 0.125 * density
    total = jnp.float32(0.0)
    for offsets in CORNERS:
        total = total + jnp.pad(share, ((offsets[0], 1 - offsets[0]), (offsets[1], 1 - offsets[1]), (offsets[2], 1 - offsets[2])))
    return total


def element_mean(vel):
    total = jnp.float32(0.0)
    for offsets in CORNERS:
        total = total + corner(vel, offsets)
    return 0.125 * total


def selection(route_row, boxes, capacity):
    hits = route_row[None, :] == boxes[:, None]
    rank = jnp.cumsum(hits.astype(jnp.int32), axis=1) - 1
    chosen = hits[:, None, :] & (rank[:, None, :] == jnp.arange(capacity, dtype=jnp.int32)[None, :, None])
    return chosen.astype(jnp.float32)


def pair_forces(first, second, valid_first, valid_second):
    diff = first[:, :, :, None] - second[:, :, None, :]
    dist = jnp.sum(diff * diff, axis=1)
    weight = REPULSION * jnp.exp(-dist / KERNEL_SCALE) * (valid_first * valid_second)[:, None, None]
    return jnp.sum(diff * weight[:, None, :, :], axis=3)


def owner_forces(received, valid, pair_list):
    first = received[pair_list[:, 0]]
    second = received[pair_list[:, 1]]
    forces = pair_forces(first, second, valid[pair_list[:, 0]], valid[pair_list[:, 1]])
    onehot = (pair_list[:, 0][:, None] == jnp.arange(received.shape[0], dtype=jnp.int32)[None, :]).astype(jnp.float32)
    return jnp.einsum('pk,pxn->kxn', onehot, forces, precision=HIGHEST)


def reference(stiffness, density, load, alive, surf_coords, surf_nodes, routes, pairs):
    devices = N_GX * N_GY * N_GZ
    columns = N_GX * N_GY
    capacity = max(SB // 4, SB // N_GZ)
    nodes_shape = (3, NX + 1, NY + 1, NZ + 1)
    mass = node_mass(density)
    disp = jnp.zeros(nodes_shape, jnp.float32)
    vel = jnp.zeros(nodes_shape, jnp.float32)
    earlier = disp
    owner = jnp.arange(BLOCKS, dtype=jnp.int32) // SB
    index_x = owner // (N_GY * N_GZ)
    index_y = (owner // N_GZ) % N_GY
    index_z = owner % N_GZ
    local_i = surf_nodes // (CY * CZ)
    local_j = (surf_nodes // CZ) % CY
    local_k = surf_nodes % CZ
    global_i = index_x[:, None] * CX + local_i
    global_j = index_y[:, None] * CY + local_j
    global_k = index_z[:, None] * CZ + local_k
    flat_ids = (global_i * (NY + 1) + global_j) * (NZ + 1) + global_k
    boxes = jnp.arange(N_GZ, dtype=jnp.int32)
    for step in range(STEPS):
        lagged = earlier.reshape(3, -1)
        positions = jnp.moveaxis(lagged[:, flat_ids], 0, 1) + surf_coords
        positions = positions.reshape(devices, SB, 3, BNODES)
        route_rows = routes[step].reshape(devices, SB)
        chosen = jax.vmap(lambda row: selection(row, boxes, capacity))(route_rows)
        send = jnp.einsum('dbks,dsxn->dbkxn', chosen, positions, precision=HIGHEST)
        valid = jnp.sum(chosen, axis=3)
        send = send.reshape(columns, N_GZ, N_GZ, capacity, 3, BNODES).transpose(0, 2, 1, 3, 4, 5)
        send = send.reshape(devices, N_GZ * capacity, 3, BNODES)
        valid = valid.reshape(columns, N_GZ, N_GZ, capacity).transpose(0, 2, 1, 3).reshape(devices, N_GZ * capacity)
        slot_force = lax.map(lambda item: owner_forces(item[0], item[1], item[2]), (send, valid, pairs[step]))
        back = slot_force.reshape(columns, N_GZ, N_GZ, capacity, 3, BNODES).transpose(0, 2, 1, 3, 4, 5)
        back = back.reshape(devices, N_GZ, capacity, 3, BNODES)
        block_force = jnp.einsum('dbks,dbkxn->dsxn', chosen, back, precision=HIGHEST)
        block_force = jnp.moveaxis(block_force.reshape(BLOCKS, 3, BNODES), 1, 0)
        contact = jnp.zeros((3, lagged.shape[1]), jnp.float32).at[:, flat_ids].add(block_force)
        modulus = stiffness * alive[step].astype(jnp.float32)
        force = node_forces(element_stress(disp, modulus), load) + contact.reshape(nodes_shape)
        vel = vel + TIME_STEP * force / mass[None]
        earlier = disp
        disp = disp + TIME_STEP * vel
    final_modulus = stiffness * alive[STEPS - 1].astype(jnp.float32)
    return element_mean(vel), element_stress(disp, final_modulus)
```

```python
import functools
import math

import jax
import jax.numpy as jnp
from jax import lax
from jax.experimental import pallas as pl
from jax.experimental.pallas import tpu as pltpu
from jax.sharding import PartitionSpec as P

REPULSION = 1.0
KERNEL_SCALE = 0.08
TIME_STEP = 0.2
HIGHEST = lax.Precision.HIGHEST
MESH = pl.DeviceIdType.MESH
F32 = jnp.float32
BF16 = jnp.bfloat16
STRETCH = math.sqrt(math.log2(math.e) / KERNEL_SCALE)


def iota(shape, dim):
    return lax.broadcasted_iota(jnp.int32, shape, dim)


def hdot(a, b):
    return jnp.dot(a, b, preferred_element_type=F32, precision=HIGHEST)


def split2(x):
    high = x.astype(BF16)
    return high, (x - high.astype(F32)).astype(BF16)


def sum_x(q):
    return jnp.concatenate([q[:1], q[:-1] + q[1:], q[-1:]], axis=0)


def diff_x(q):
    return jnp.concatenate([-q[:1], q[:-1] - q[1:], q[-1:]], axis=0)


def body(sizes, stiff_ref, dens_ref, load_ref, alive_ref, coords_ref, nodes_ref, routes_ref, pairt_ref, pair_ref,
         vout_ref, sout_ref, *scratch):
    (mod, big_f, rim_f, load_f, load_r, vel, vel_r, disp, disp_r, minv, minv_r, route_all, pos_all, slots, second,
     partial, send_f, ret, back_pick, rank_in, gather_w, lane_pick, scatter_w, scatter_l,
     x_send, x_recv, y_send, y_recv, z_send, z_recv,
     route_ss, route_rs, pos_ss, pos_rs, ret_ss, ret_rs, x_ss, x_rs, y_ss, y_rs, z_ss, z_rs) = scratch
    count_x, count_y, cx, cy, cz, sb, npair, steps, nz, cap = sizes
    nx = cx + 1
    rows = 16
    ix, iy, iz = lax.axis_index("gx"), lax.axis_index("gy"), lax.axis_index("gz")
    lanes = iota((rows, cz), 1)
    lane3 = iota((1, 1, cz), 2)

    def roll(v, shift, axis):
        return pltpu.roll(v, shift % v.shape[axis], axis)

    for ref in (x_send, x_recv, y_send, y_recv, z_send, z_recv, mod, slots, send_f):
        ref[...] = jnp.zeros(ref.shape, ref.dtype)

    sides = (("gx", ix, count_x), ("gy", iy, count_y), ("gz", iz, nz))
    barrier = pltpu.get_barrier_semaphore()
    expect = jnp.int32(nz - 1)
    for name, at, count in sides[:2]:
        @pl.when(at > 0)
        def _():
            pl.semaphore_signal(barrier, inc=1, device_id={name: at - 1}, device_id_type=MESH)

        @pl.when(at < count - 1)
        def _():
            pl.semaphore_signal(barrier, inc=1, device_id={name: at + 1}, device_id_type=MESH)
        expect = expect + jnp.where(at > 0, 1, 0) + jnp.where(at < count - 1, 1, 0)
    for other in range(1, nz):
        pl.semaphore_signal(barrier, inc=1, device_id={"gz": lax.rem(iz + other, nz)}, device_id_type=MESH)
    pl.semaphore_wait(barrier, expect)

    def column(send_ref, recv_ref, ss, rs):
        out = []
        for other in range(1, nz):
            to = lax.rem(iz + other, nz)
            out.append(pltpu.make_async_remote_copy(
                src_ref=send_ref(to), dst_ref=recv_ref, send_sem=ss.at[other - 1], recv_sem=rs.at[other - 1],
                device_id={"gz": to}, device_id_type=MESH))
        return out

    def pos_copies(phase):
        return column(lambda to: pos_all.at[phase, iz], pos_all.at[phase, iz], pos_ss.at[phase], pos_rs.at[phase])

    def ret_copies(t):
        return column(lambda to: send_f.at[t, to], ret.at[t, iz], ret_ss.at[t], ret_rs.at[t])

    route_copies = column(lambda to: route_all.at[iz], route_all.at[iz], route_ss, route_rs)

    route_all[iz] = jnp.full((8, 128), -1, jnp.int32)
    route_all[iz, 0:steps, 0:sb] = routes_ref[...]
    for x in range(3):
        pos_all[0, iz, :, x * 128:(x + 1) * 128] = coords_ref[:, x, :]
    for c in route_copies + pos_copies(0):
        c.start()

    for t in range(steps):
        mod[t, :, 0:cy, :] = stiff_ref[...] * alive_ref[t].astype(F32)
    for c in range(4):
        mod[steps + c, :, 0:cy, :] = 0.125 * (load_ref[c] if c < 3 else dens_ref[...])
    rim = jnp.zeros((rows, cz), F32)
    for c in range(4):
        q = sum_x(mod[steps + c])
        q = q + roll(q, 1, 1)
        r = roll(q, 1, 2)
        load_f[c] = q + jnp.where(lane3 > 0, r, 0.0)
        for i in range(nx):
            at = c * nx + i
            rim = rim + jnp.where(lanes == at, roll(r[i], at, 1), 0.0)
    load_r[...] = rim

    ids = nodes_ref[...]
    row = lax.shift_right_logical(ids, jnp.full(ids.shape, cz.bit_length() - 1, jnp.int32))
    lane = ids & (cz - 1)
    wide = row
    for m in range(1, cx):
        wide = wide + jnp.where(row >= cy * m, rows - cy, 0)
    depth = cx * rows
    wide_pad = jnp.concatenate([wide.astype(F32), jnp.zeros((128 - sb, 128), F32)], axis=0)
    wide_t = jnp.transpose(wide_pad)
    for s in range(sb):
        hot = (iota((depth, 128), 0) == wide[s:s + 1, :]).astype(F32).astype(BF16)
        gather_w[0:depth, s * 128:(s + 1) * 128] = hot
        gather_w[depth:2 * depth, s * 128:(s + 1) * 128] = hot
        lane_pick[s] = (iota((cz, 128), 0) == lane[s:s + 1, :]).astype(F32)
        col = jnp.broadcast_to(wide_t[:, s:s + 1], (128, depth))
        hot = (iota((128, depth), 1).astype(F32) == col).astype(F32).astype(BF16)
        scatter_w[s * 256:s * 256 + 128, :] = hot
        scatter_w[s * 256 + 128:s * 256 + 256, :] = hot

    def wait_all(copies):
        for c in copies:
            c.wait()

    wait_all(route_copies)
    upper = (iota((128, 128), 0) <= iota((128, 128), 1)).astype(F32)
    own = route_all[iz]
    for b in range(nz):
        hits = (route_all[b] == iz).astype(F32)
        rank_in[b] = jnp.where(hits > 0, jnp.dot(hits, upper, preferred_element_type=F32), 0.0)
    slot8 = nz * 8
    picks = []
    for b in range(nz):
        hits = (own == b).astype(F32)
        picks.append(jnp.where(hits > 0, jnp.dot(hits, upper, preferred_element_type=F32), 0.0))
    ranks8 = (iota((8, 128), 0) + 1).astype(F32)
    live8 = iota((8, 128), 0) < cap
    for t in range(steps):
        parts = [jnp.where((picks[b][t:t + 1, :] == ranks8) & live8, 1.0, 0.0) for b in range(nz)]
        table = jnp.concatenate(parts + [jnp.zeros((128 - slot8, 128), F32)], axis=0)
        back_pick[t] = jnp.transpose(table)[0:sb, :]

    def gather(phase):
        highs, lows = [], []
        for c in range(3):
            flat = jnp.transpose(disp[c, 0:cx].reshape(depth, cz))
            high, low = split2(flat)
            highs.append(high)
            lows.append(low)
        left = jnp.concatenate([jnp.concatenate(highs, axis=0), jnp.concatenate(lows, axis=0)], axis=1)
        for s in range(0, sb, 2):
            got = jnp.dot(left, gather_w[:, s * 128:(s + 2) * 128], preferred_element_type=F32)
            for h in range(2):
                for c in range(3):
                    part = got[c * cz:(c + 1) * cz, h * 128:(h + 1) * 128] * lane_pick[s + h]
                    pos_all[phase, iz, s + h:s + h + 1, c * 128:(c + 1) * 128] = (
                        jnp.sum(part, axis=0, keepdims=True) + coords_ref[s + h, c:c + 1, :])

    def build_slots(t, phase):
        live = []
        for b in range(nz):
            hot = jnp.where(rank_in[b, t:t + 1, :] == ranks8[0:cap], 1.0, 0.0)
            live.append(jnp.sum(hot, axis=1, keepdims=True))
            got = STRETCH * hdot(hot[:, 0:sb], pos_all[phase, b])
            for x in range(3):
                slots[x, b * cap:(b + 1) * cap, :] = got[:, x * 128:(x + 1) * 128]
        for x in range(3):
            flipped = jnp.transpose(slots[x])
            for k in range(nz * cap):
                second[k, x] = jnp.broadcast_to(flipped[:, k:k + 1], (128, 128))
        return live

    def pair_range(t, start, stop):
        def one(q, carry):
            p = pair_ref[t * npair * 2 + q * 2]
            r = pair_ref[t * npair * 2 + q * 2 + 1]
            xi = [jnp.broadcast_to(slots[x, pl.ds(p, 1), :], (8, 128)) for x in range(3)]
            acc = [jnp.zeros((8, 128), F32)] * 3
            for j in range(16):
                d = [xi[x] - second[r, x, j * 8:(j + 1) * 8, :] for x in range(3)]
                w = jnp.exp2(-(d[0] * d[0] + d[1] * d[1] + d[2] * d[2]))
                acc = [acc[x] + d[x] * w for x in range(3)]
            for x in range(3):
                partial[x, pl.ds(q, 1), :] = jnp.sum(acc[x], axis=0, keepdims=True)
            return carry
        lax.fori_loop(start, stop, one, 0)

    def finish_pairs(t, live):
        first = pairt_ref[t, 0:1, :]
        other = pairt_ref[t, 1:2, :]
        live_p = jnp.zeros((1, npair), F32)
        live_r = jnp.zeros((1, npair), F32)
        for b in range(nz):
            slot = iota((cap, npair), 0) + b * cap
            live_p = live_p + jnp.sum(jnp.where(first == slot, live[b], 0.0), axis=0, keepdims=True)
            live_r = live_r + jnp.sum(jnp.where(other == slot, live[b], 0.0), axis=0, keepdims=True)
        weight = live_p * live_r * (REPULSION / STRETCH)
        for b in range(nz):
            hot = jnp.where(first == iota((cap, npair), 0) + b * cap, weight, 0.0)
            for x in range(3):
                send_f[t, b, 0:cap, x * 128:(x + 1) * 128] = hdot(hot, partial[x])
        for c in ret_copies(t):
            c.start()
        ret[t, iz] = send_f[t, iz]

    def scatter(t):
        wait_all(ret_copies(t))
        force = hdot(back_pick[t, :, 0:slot8], ret[t].reshape(slot8, 384))
        for c in range(3):
            for s in range(sb):
                line = force[s:s + 1, c * 128:(c + 1) * 128]
                spread = lane_pick[s] * line
                high, low = split2(spread)
                scatter_l[c * cz:(c + 1) * cz, s * 256:s * 256 + 128] = high
                scatter_l[c * cz:(c + 1) * cz, s * 256 + 128:s * 256 + 256] = low
        total = jnp.dot(scatter_l[...], scatter_w[...], preferred_element_type=F32)
        for c in range(3):
            grid = jnp.transpose(total[c * cz:(c + 1) * cz, :]).reshape(cx, rows, cz)
            big_f[c, 0:cx] = big_f[c, 0:cx] + grid

    def corners(field, rim_value, c):
        u = field[c]
        edge = jnp.stack([roll(rim_value, -(c * nx + i), 1) for i in range(nx)])
        above = roll(jnp.where(lane3 == 0, edge, u), -1, 2)
        both = u + above
        step = above - u
        shifted = roll(both, -1, 1)
        return both + shifted, shifted - both, step + roll(step, -1, 1)

    def stress_of(modulus):
        grads = []
        rim_value = disp_r[...]
        for c in range(3):
            mean, along_y, along_z = corners(disp, rim_value, c)
            grads.append((0.25 * (mean[1:] - mean[:-1]), 0.25 * (along_y[1:] + along_y[:-1]),
                          0.25 * (along_z[1:] + along_z[:-1])))
        trace = grads[0][0] + grads[1][1] + grads[2][2]
        return (modulus * (2.0 * grads[0][0] + trace), modulus * (2.0 * grads[1][1] + trace),
                modulus * (2.0 * grads[2][2] + trace), modulus * (grads[0][1] + grads[1][0]),
                modulus * (grads[1][2] + grads[2][1]), modulus * (grads[0][2] + grads[2][0]))

    def internal(t):
        s = stress_of(mod[t])
        table = ((s[0], s[3], s[5]), (s[3], s[1], s[4]), (s[5], s[4], s[2]))
        rim = load_r[...]
        for c in range(3):
            a0 = -0.25 * diff_x(table[c][0])
            ay = -0.25 * sum_x(table[c][1])
            az = -0.25 * sum_x(table[c][2])
            a = (a0 - ay) + roll(a0 + ay, 1, 1)
            b = az + roll(az, 1, 1)
            r = roll(a + b, 1, 2)
            big_f[c] = load_f[c] + (a - b) + jnp.where(lane3 > 0, r, 0.0)
            for i in range(nx):
                at = c * nx + i
                rim = rim + jnp.where(lanes == at, roll(r[i], at, 1), 0.0)
        rim_f[...] = rim

    def axis_copies(side, send, recv, ss, rs, t, used):
        name, at, count = side
        out = []
        for way, to, sends, gets in ((0, at - 1, at > 0, at < count - 1), (1, at + 1, at < count - 1, at > 0)):
            out.append((pltpu.make_async_remote_copy(
                src_ref=send.at[t, way, 0:used], dst_ref=recv.at[t, way, 0:used], send_sem=ss.at[t, way],
                recv_sem=rs.at[t, way], device_id={name: to}, device_id_type=MESH), sends, gets))
        return out

    def start(copies):
        for copy, sends, _ in copies:
            @pl.when(sends)
            def _():
                copy.start()

    def finish(copies):
        for copy, sends, gets in copies:
            @pl.when(sends)
            def _():
                copy.wait_send()

            @pl.when(gets)
            def _():
                copy.wait_recv()

    def halo(t, fillers):
        comps = 4 if t == 0 else 3
        low_lane = functools.reduce(jnp.logical_or, [lanes == c * nx for c in range(4)])
        high_lane = functools.reduce(jnp.logical_or, [lanes == c * nx + cx for c in range(4)])
        for way, plane in ((0, 0), (1, cx)):
            x_send[t, way, 0] = rim_f[...]
            for c in range(comps):
                x_send[t, way, 1 + c] = big_f[c, plane]
        copies = axis_copies(sides[0], x_send, x_recv, x_ss, x_rs, t, comps + 1)
        start(copies)
        fillers[0]()
        finish(copies)
        for c in range(comps):
            big_f[c, 0] = big_f[c, 0] + x_recv[t, 1, 1 + c]
            big_f[c, cx] = big_f[c, cx] + x_recv[t, 0, 1 + c]
        rim_f[...] = (rim_f[...] + jnp.where(low_lane, roll(x_recv[t, 1, 0], -cx, 1), 0.0)
                      + jnp.where(high_lane, roll(x_recv[t, 0, 0], cx, 1), 0.0))

        used = -(-(1 + comps * nx) // 8) * 8
        for way, line in ((0, 0), (1, cy)):
            y_send[t, way, 0:1] = rim_f[line:line + 1]
            for c in range(comps):
                for i in range(nx):
                    at = 1 + c * nx + i
                    y_send[t, way, at:at + 1] = big_f[c, i, line:line + 1]
        copies = axis_copies(sides[1], y_send, y_recv, y_ss, y_rs, t, used)
        start(copies)
        fillers[1]()
        finish(copies)
        for way, line in ((1, 0), (0, cy)):
            rim_f[line:line + 1] = rim_f[line:line + 1] + y_recv[t, way, 0:1]
            for c in range(comps):
                for i in range(nx):
                    at = 1 + c * nx + i
                    big_f[c, i, line:line + 1] = big_f[c, i, line:line + 1] + y_recv[t, way, at:at + 1]

        packed = jnp.zeros((rows, cz), F32)
        for c in range(comps):
            for i in range(nx):
                at = c * nx + i
                packed = jnp.where(lanes == at, roll(big_f[c, i], at, 1), packed)
        z_send[t, 0] = packed
        z_send[t, 1] = rim_f[...]
        copies = axis_copies(sides[2], z_send, z_recv, z_ss, z_rs, t, rows)
        start(copies)
        fillers[2]()
        finish(copies)
        rim_f[...] = rim_f[...] + z_recv[t, 0]
        below = z_recv[t, 1]
        for c in range(comps):
            for i in range(nx):
                at = c * nx + i
                big_f[c, i] = big_f[c, i] + jnp.where(lanes == 0, roll(below, -at, 1), 0.0)

    def contact(t):
        cuts = [0, npair // 3, 2 * npair // 3, npair]
        return [lambda lo=lo, hi=hi: pair_range(t, lo, hi) for lo, hi in zip(cuts[:-1], cuts[1:])]

    nothing = [lambda: None] * 3

    wait_all(pos_copies(0))
    live = build_slots(0, 0)
    pair_range(0, 0, npair)
    finish_pairs(0, live)

    for t in range(steps):
        if t == 0:
            big_f[...] = load_f[...]
            rim_f[...] = load_r[...]
        else:
            if t + 1 < steps:
                gather(t)
                for c in pos_copies(t):
                    c.start()
            internal(t)
        scatter(t)
        if t + 1 < steps:
            if t > 0:
                wait_all(pos_copies(t))
            live = build_slots(t + 1, t)
            halo(t, contact(t + 1))
            finish_pairs(t + 1, live)
        else:
            halo(t, nothing)
        if t == 0:
            mass = big_f[3]
            minv[...] = jnp.where(mass > 0.0, 1.0 / mass, 0.0)
            held = jnp.where((lanes >= 3 * nx) & (lanes < 4 * nx), rim_f[...], 0.0)
            spread = roll(held, -3 * nx, 1) + roll(held, -2 * nx, 1) + roll(held, -nx, 1)
            minv_r[...] = jnp.where(spread > 0.0, 1.0 / spread, 0.0)
            for c in range(3):
                vel[c] = TIME_STEP * (big_f[c] * minv[...])
            vel_r[...] = TIME_STEP * (rim_f[...] * minv_r[...])
            disp[...] = TIME_STEP * vel[...]
            disp_r[...] = TIME_STEP * vel_r[...]
        else:
            for c in range(3):
                vel[c] = vel[c] + TIME_STEP * (big_f[c] * minv[...])
            vel_r[...] = vel_r[...] + TIME_STEP * (rim_f[...] * minv_r[...])
            disp[...] = disp[...] + TIME_STEP * vel[...]
            disp_r[...] = disp_r[...] + TIME_STEP * vel_r[...]

    rim_value = vel_r[...]
    for c in range(3):
        mean, _, _ = corners(vel, rim_value, c)
        vout_ref[c] = (0.125 * (mean[1:] + mean[:-1]))[:, 0:cy, :]
    s = stress_of(mod[steps - 1])
    for c in range(6):
        sout_ref[c] = s[c][:, 0:cy, :]


def per_device(stiffness, density, load, alive, surf_coords, surf_nodes, routes, pairs):
    cx, cy, cz = stiffness.shape
    steps = alive.shape[0]
    sb = surf_coords.shape[0]
    npair = pairs.shape[2]
    count_x, count_y, nz = (lax.axis_size(a) for a in ("gx", "gy", "gz"))
    cap = max(sb // 4, sb // nz)
    nx = cx + 1
    pairt = jnp.transpose(pairs[:, 0], (0, 2, 1))
    sizes = (count_x, count_y, cx, cy, cz, sb, npair, steps, nz, cap)
    vm = lambda *shape: pltpu.VMEM(shape, F32)
    dma = lambda *shape: pltpu.SemaphoreType.DMA(shape)
    column = max(nz - 1, 1)
    scratch = [
        vm(steps + 4, cx, 16, cz), vm(4, nx, 16, cz), vm(16, cz), vm(4, nx, 16, cz), vm(16, cz),
        vm(3, nx, 16, cz), vm(16, cz), vm(3, nx, 16, cz), vm(16, cz), vm(nx, 16, cz), vm(16, cz),
        pltpu.VMEM((nz, 8, 128), jnp.int32), vm(steps - 1, nz, sb, 384), vm(3, 128, 128), vm(nz * cap, 3, 128, 128),
        vm(3, npair, 128), vm(steps, nz, 8, 384), vm(steps, nz, 8, 384), vm(steps, sb, 128), vm(nz, 8, 128),
        pltpu.VMEM((2 * cx * 16, sb * 128), BF16), vm(sb, cz, 128), pltpu.VMEM((2 * sb * 128, cx * 16), BF16),
        pltpu.VMEM((3 * cz, 2 * sb * 128), BF16),
        vm(steps, 2, 5, 16, cz), vm(steps, 2, 5, 16, cz), vm(steps, 2, 40, cz), vm(steps, 2, 40, cz),
        vm(steps, 2, 16, cz), vm(steps, 2, 16, cz),
        dma(column), dma(column), dma(steps - 1, column), dma(steps - 1, column), dma(steps, column), dma(steps, column),
        dma(steps, 2), dma(steps, 2), dma(steps, 2), dma(steps, 2), dma(steps, 2), dma(steps, 2),
    ]
    vmem = pl.BlockSpec(memory_space=pltpu.VMEM)
    return pl.pallas_call(
        functools.partial(body, sizes),
        out_shape=(jax.ShapeDtypeStruct((3, cx, cy, cz), F32), jax.ShapeDtypeStruct((6, cx, cy, cz), F32)),
        in_specs=[vmem] * 8 + [pl.BlockSpec(memory_space=pltpu.SMEM)],
        out_specs=(vmem, vmem),
        scratch_shapes=scratch,
        compiler_params=pltpu.CompilerParams(collective_id=0, has_side_effects=True, vmem_limit_bytes=56 * 1024 * 1024),
    )(stiffness, density, load, alive, surf_coords, surf_nodes, routes, pairt, pairs.reshape(-1))


def solution(mesh):
    return jax.shard_map(
        per_device,
        mesh=mesh,
        in_specs=(
            P("gx", "gy", "gz"),
            P("gx", "gy", "gz"),
            P(None, "gx", "gy", "gz"),
            P(None, "gx", "gy", "gz"),
            P(("gx", "gy", "gz"), None, None),
            P(("gx", "gy", "gz"), None),
            P(None, ("gx", "gy", "gz")),
            P(None, ("gx", "gy", "gz"), None, None),
        ),
        out_specs=(P(None, "gx", "gy", "gz"), P(None, "gx", "gy", "gz")),
        check_vma=False,
    )
```

```python
import functools
import math

import jax
import jax.numpy as jnp
from jax import lax
from jax.experimental import pallas as pl
from jax.experimental.pallas import tpu as pltpu
from jax.sharding import PartitionSpec as P

REPULSION = 1.0
KERNEL_SCALE = 0.08
TIME_STEP = 0.2
HIGHEST = lax.Precision.HIGHEST
MESH = pl.DeviceIdType.MESH
F32 = jnp.float32
BF16 = jnp.bfloat16
STRETCH = math.sqrt(math.log2(math.e) / KERNEL_SCALE)


def iota(shape, dim):
    return lax.broadcasted_iota(jnp.int32, shape, dim)


def hdot(a, b):
    return jnp.dot(a, b, preferred_element_type=F32, precision=HIGHEST)


def split2(x):
    high = x.astype(BF16)
    return high, (x - high.astype(F32)).astype(BF16)


def sum_x(q):
    return jnp.concatenate([q[:1], q[:-1] + q[1:], q[-1:]], axis=0)


def diff_x(q):
    return jnp.concatenate([-q[:1], q[:-1] - q[1:], q[-1:]], axis=0)


def body(sizes, stiff_ref, dens_ref, load_ref, alive_ref, coords_ref, nodes_ref, routes_ref, pairt_ref, pair_ref,
         vout_ref, sout_ref, *scratch):
    (mod, big_f, rim_f, load_f, load_r, vel, vel_r, disp, disp_r, minv, minv_r, route_all, pos_all, slots, second,
     partial, send_f, ret, back_pick, rank_in, gather_w, lane_pick, lane_pick_h, touch, scatter_w, scatter_l,
     x_send, x_recv, y_send, y_recv, z_send, z_recv,
     route_ss, route_rs, pos_ss, pos_rs, ret_ss, ret_rs, x_ss, x_rs, y_ss, y_rs, z_ss, z_rs) = scratch
    count_x, count_y, cx, cy, cz, sb, npair, steps, nz, cap = sizes
    nx = cx + 1
    rows = 16
    ix, iy, iz = lax.axis_index("gx"), lax.axis_index("gy"), lax.axis_index("gz")
    lanes = iota((rows, cz), 1)
    lane3 = iota((1, 1, cz), 2)

    def roll(v, shift, axis):
        return pltpu.roll(v, shift % v.shape[axis], axis)

    for ref in (x_send, x_recv, y_send, y_recv, z_send, z_recv, mod, slots, send_f):
        ref[...] = jnp.zeros(ref.shape, ref.dtype)

    sides = (("gx", ix, count_x), ("gy", iy, count_y), ("gz", iz, nz))
    barrier = pltpu.get_barrier_semaphore()
    expect = jnp.int32(nz - 1)
    for name, at, count in sides[:2]:
        @pl.when(at > 0)
        def _():
            pl.semaphore_signal(barrier, inc=1, device_id={name: at - 1}, device_id_type=MESH)

        @pl.when(at < count - 1)
        def _():
            pl.semaphore_signal(barrier, inc=1, device_id={name: at + 1}, device_id_type=MESH)
        expect = expect + jnp.where(at > 0, 1, 0) + jnp.where(at < count - 1, 1, 0)
    for other in range(1, nz):
        pl.semaphore_signal(barrier, inc=1, device_id={"gz": lax.rem(iz + other, nz)}, device_id_type=MESH)
    pl.semaphore_wait(barrier, expect)

    def column(send_ref, recv_ref, ss, rs):
        out = []
        for other in range(1, nz):
            to = lax.rem(iz + other, nz)
            out.append(pltpu.make_async_remote_copy(
                src_ref=send_ref(to), dst_ref=recv_ref, send_sem=ss.at[other - 1], recv_sem=rs.at[other - 1],
                device_id={"gz": to}, device_id_type=MESH))
        return out

    def pos_copies(phase):
        return column(lambda to: pos_all.at[phase, iz], pos_all.at[phase, iz], pos_ss.at[phase], pos_rs.at[phase])

    def ret_copies(t):
        return column(lambda to: send_f.at[t, to], ret.at[t, iz], ret_ss.at[t], ret_rs.at[t])

    route_copies = column(lambda to: route_all.at[iz], route_all.at[iz], route_ss, route_rs)

    route_all[iz] = jnp.full((8, 128), -1, jnp.int32)
    route_all[iz, 0:steps, 0:sb] = routes_ref[...]
    for x in range(3):
        pos_all[0, iz, :, x * 128:(x + 1) * 128] = coords_ref[x]
    for c in route_copies + pos_copies(0):
        c.start()

    for t in range(steps):
        for i in range(cx):
            mod[t, i, 0:cy, :] = stiff_ref[:, i, :] * alive_ref[t, :, i, :].astype(F32)
    for c in range(4):
        for i in range(cx):
            mod[steps + c, i, 0:cy, :] = 0.125 * (load_ref[c, :, i, :] if c < 3 else dens_ref[:, i, :])
    rim = jnp.zeros((rows, cz), F32)
    for c in range(4):
        q = sum_x(mod[steps + c])
        q = q + roll(q, 1, 1)
        r = roll(q, 1, 2)
        load_f[c] = q + jnp.where(lane3 > 0, r, 0.0)
        for i in range(nx):
            at = c * nx + i
            rim = rim + jnp.where(lanes == at, roll(r[i], at, 1), 0.0)
    load_r[...] = rim

    ids = nodes_ref[...]
    row = lax.shift_right_logical(ids, jnp.full(ids.shape, cz.bit_length() - 1, jnp.int32))
    lane = ids & (cz - 1)
    wide = row
    for m in range(1, cx):
        wide = wide + jnp.where(row >= cy * m, rows - cy, 0)
    depth = cx * rows
    wide_pad = jnp.concatenate([wide.astype(F32), jnp.zeros((128 - sb, 128), F32)], axis=0)
    wide_t = jnp.transpose(wide_pad)
    for s in range(sb):
        hot = (iota((depth, 128), 0) == wide[s:s + 1, :]).astype(F32).astype(BF16)
        gather_w[s, 0:depth, :] = hot
        gather_w[s, depth:2 * depth, :] = hot
        pick = (iota((cz, 128), 0) == lane[s:s + 1, :]).astype(F32)
        lane_pick[s] = pick
        lane_pick_h[s] = pick.astype(BF16)
        col = jnp.broadcast_to(wide_t[:, s:s + 1], (128, depth))
        hot = (iota((128, depth), 1).astype(F32) == col).astype(F32).astype(BF16)
        scatter_w[s * 256:s * 256 + 128, :] = hot
        scatter_w[s * 256 + 128:s * 256 + 256, :] = hot

    def wait_all(copies):
        for c in copies:
            c.wait()

    wait_all(route_copies)
    upper = (iota((128, 128), 0) <= iota((128, 128), 1)).astype(F32)
    own = route_all[iz]
    for b in range(nz):
        hits = (route_all[b] == iz).astype(F32)
        rank_in[b] = jnp.where(hits > 0, jnp.dot(hits, upper, preferred_element_type=F32), 0.0)
    slot8 = nz * 8
    picks = []
    for b in range(nz):
        hits = (own == b).astype(F32)
        picks.append(jnp.where(hits > 0, jnp.dot(hits, upper, preferred_element_type=F32), 0.0))
    ranks8 = (iota((8, 128), 0) + 1).astype(F32)
    live8 = iota((8, 128), 0) < cap
    for t in range(steps):
        parts = [jnp.where((picks[b][t:t + 1, :] == ranks8) & live8, 1.0, 0.0) for b in range(nz)]
        table = jnp.concatenate(parts + [jnp.zeros((128 - slot8, 128), F32)], axis=0)
        back_pick[t] = jnp.transpose(table)[0:sb, :]

    def gather(phase):
        highs, lows = [], []
        for c in range(3):
            flat = jnp.transpose(disp[c, 0:cx].reshape(depth, cz))
            high, low = split2(flat)
            highs.append(high)
            lows.append(low)
        left = jnp.concatenate([jnp.concatenate(highs, axis=0), jnp.concatenate(lows, axis=0)], axis=1)
        for s in range(0, sb, 2):
            got = jnp.dot(left, jnp.concatenate([gather_w[s], gather_w[s + 1]], axis=1), preferred_element_type=F32)
            for h in range(2):
                for c in range(3):
                    part = got[c * cz:(c + 1) * cz, h * 128:(h + 1) * 128] * lane_pick[s + h]
                    pos_all[phase, iz, s + h:s + h + 1, c * 128:(c + 1) * 128] = (
                        jnp.sum(part, axis=0, keepdims=True) + coords_ref[c, s + h:s + h + 1, :])

    def build_slots(t, phase):
        live = []
        for b in range(nz):
            hot = jnp.where(rank_in[b, t:t + 1, :] == ranks8[0:cap], 1.0, 0.0)
            live.append(jnp.sum(hot, axis=1, keepdims=True))
            got = STRETCH * hdot(hot[:, 0:sb], pos_all[phase, b])
            for x in range(3):
                slots[x, b * cap:(b + 1) * cap, :] = got[:, x * 128:(x + 1) * 128]
        for x in range(3):
            flipped = jnp.transpose(slots[x])
            for k in range(nz * cap):
                second[k, x] = jnp.broadcast_to(flipped[:, k:k + 1], (128, 128))
        return live

    unroll = 4

    def pair_range(t, start, stop):
        def some(at, carry):
            for u in range(unroll):
                one(start + at * unroll + u)
            return carry

        def one(q):
            p = pair_ref[t, 0, q]
            r = pair_ref[t, 1, q]
            xi = [jnp.broadcast_to(slots[x, pl.ds(p, 1), :], (8, 128)) for x in range(3)]
            acc = [jnp.zeros((8, 128), F32)] * 3
            for j in range(16):
                d = [xi[x] - second[r, x, j * 8:(j + 1) * 8, :] for x in range(3)]
                w = jnp.exp2(-(d[0] * d[0] + d[1] * d[1] + d[2] * d[2]))
                acc = [acc[x] + d[x] * w for x in range(3)]
            for x in range(3):
                partial[x, pl.ds(q, 1), :] = jnp.sum(acc[x], axis=0, keepdims=True)
        lax.fori_loop(0, (stop - start) // unroll, some, 0)

    def finish_pairs(t, live):
        first = pairt_ref[t, 0:1, :]
        other = pairt_ref[t, 1:2, :]
        live_p = jnp.zeros((1, npair), F32)
        live_r = jnp.zeros((1, npair), F32)
        for b in range(nz):
            slot = iota((cap, npair), 0) + b * cap
            live_p = live_p + jnp.sum(jnp.where(first == slot, live[b], 0.0), axis=0, keepdims=True)
            live_r = live_r + jnp.sum(jnp.where(other == slot, live[b], 0.0), axis=0, keepdims=True)
        weight = live_p * live_r * (REPULSION / STRETCH)
        for b in range(nz):
            hot = jnp.where(first == iota((cap, npair), 0) + b * cap, weight, 0.0)
            for x in range(3):
                send_f[t, b, 0:cap, x * 128:(x + 1) * 128] = hdot(hot, partial[x])
        for c in ret_copies(t):
            c.start()
        ret[t, iz] = send_f[t, iz]

    def scatter(t):
        wait_all(ret_copies(t))
        force = hdot(back_pick[t, :, 0:slot8], ret[t].reshape(slot8, 384))
        for c in range(3):
            for s in range(sb):
                line = jnp.broadcast_to(force[s:s + 1, c * 128:(c + 1) * 128], (16, 128))
                for h, half in enumerate(split2(line)):
                    spread = lane_pick_h[s].reshape(cz // 16, 16, 128) * half[None]
                    scatter_l[2 * s + h, c * cz:(c + 1) * cz, :] = spread.reshape(cz, 128)
        left = jnp.concatenate([scatter_l[k] for k in range(2 * sb)], axis=1)
        total = jnp.dot(left, scatter_w[...], preferred_element_type=F32)
        for c in range(3):
            grid = jnp.transpose(total[c * cz:(c + 1) * cz, :]).reshape(cx, rows, cz)
            touch[c] = grid

    def corners(field, rim_value, c):
        u = field[c]
        edge = jnp.stack([roll(rim_value, -(c * nx + i), 1) for i in range(nx)])
        above = roll(jnp.where(lane3 == 0, edge, u), -1, 2)
        both = u + above
        step = above - u
        shifted = roll(both, -1, 1)
        return both + shifted, shifted - both, step + roll(step, -1, 1)

    def stress_of(modulus):
        grads = []
        rim_value = disp_r[...]
        for c in range(3):
            mean, along_y, along_z = corners(disp, rim_value, c)
            grads.append((0.25 * (mean[1:] - mean[:-1]), 0.25 * (along_y[1:] + along_y[:-1]),
                          0.25 * (along_z[1:] + along_z[:-1])))
        trace = grads[0][0] + grads[1][1] + grads[2][2]
        return (modulus * (2.0 * grads[0][0] + trace), modulus * (2.0 * grads[1][1] + trace),
                modulus * (2.0 * grads[2][2] + trace), modulus * (grads[0][1] + grads[1][0]),
                modulus * (grads[1][2] + grads[2][1]), modulus * (grads[0][2] + grads[2][0]))

    def internal(t):
        s = stress_of(mod[t])
        table = ((s[0], s[3], s[5]), (s[3], s[1], s[4]), (s[5], s[4], s[2]))
        rim = load_r[...]
        for c in range(3):
            a0 = -0.25 * diff_x(table[c][0])
            ay = -0.25 * sum_x(table[c][1])
            az = -0.25 * sum_x(table[c][2])
            a = (a0 - ay) + roll(a0 + ay, 1, 1)
            b = az + roll(az, 1, 1)
            r = roll(a + b, 1, 2)
            big_f[c] = load_f[c] + (a - b) + jnp.where(lane3 > 0, r, 0.0)
            for i in range(nx):
                at = c * nx + i
                rim = rim + jnp.where(lanes == at, roll(r[i], at, 1), 0.0)
        rim_f[...] = rim

    def axis_copies(side, send, recv, ss, rs, t, used):
        name, at, count = side
        out = []
        for way, to, sends, gets in ((0, at - 1, at > 0, at < count - 1), (1, at + 1, at < count - 1, at > 0)):
            out.append((pltpu.make_async_remote_copy(
                src_ref=send.at[t, way, 0:used], dst_ref=recv.at[t, way, 0:used], send_sem=ss.at[t, way],
                recv_sem=rs.at[t, way], device_id={name: to}, device_id_type=MESH), sends, gets))
        return out

    def start(copies):
        for copy, sends, _ in copies:
            @pl.when(sends)
            def _():
                copy.start()

    def finish(copies):
        for copy, sends, gets in copies:
            @pl.when(sends)
            def _():
                copy.wait_send()

            @pl.when(gets)
            def _():
                copy.wait_recv()

    def halo(t, fillers):
        comps = 4 if t == 0 else 3
        low_lane = functools.reduce(jnp.logical_or, [lanes == c * nx for c in range(4)])
        high_lane = functools.reduce(jnp.logical_or, [lanes == c * nx + cx for c in range(4)])
        for way, plane in ((0, 0), (1, cx)):
            x_send[t, way, 0] = rim_f[...]
            for c in range(comps):
                x_send[t, way, 1 + c] = big_f[c, plane]
        copies = axis_copies(sides[0], x_send, x_recv, x_ss, x_rs, t, comps + 1)
        start(copies)
        fillers[0]()
        finish(copies)
        for c in range(comps):
            big_f[c, 0] = big_f[c, 0] + x_recv[t, 1, 1 + c]
            big_f[c, cx] = big_f[c, cx] + x_recv[t, 0, 1 + c]
        rim_f[...] = (rim_f[...] + jnp.where(low_lane, roll(x_recv[t, 1, 0], -cx, 1), 0.0)
                      + jnp.where(high_lane, roll(x_recv[t, 0, 0], cx, 1), 0.0))

        used = -(-(1 + comps * nx) // 8) * 8
        for way, line in ((0, 0), (1, cy)):
            y_send[t, way, 0:1] = rim_f[line:line + 1]
            for c in range(comps):
                for i in range(nx):
                    at = 1 + c * nx + i
                    y_send[t, way, at:at + 1] = big_f[c, i, line:line + 1]
        copies = axis_copies(sides[1], y_send, y_recv, y_ss, y_rs, t, used)
        start(copies)
        fillers[1]()
        finish(copies)
        for way, line in ((1, 0), (0, cy)):
            rim_f[line:line + 1] = rim_f[line:line + 1] + y_recv[t, way, 0:1]
            for c in range(comps):
                for i in range(nx):
                    at = 1 + c * nx + i
                    big_f[c, i, line:line + 1] = big_f[c, i, line:line + 1] + y_recv[t, way, at:at + 1]

        packed = jnp.zeros((rows, cz), F32)
        for c in range(comps):
            for i in range(nx):
                at = c * nx + i
                packed = jnp.where(lanes == at, roll(big_f[c, i], at, 1), packed)
        z_send[t, 0] = packed
        z_send[t, 1] = rim_f[...]
        copies = axis_copies(sides[2], z_send, z_recv, z_ss, z_rs, t, rows)
        start(copies)
        fillers[2]()
        finish(copies)
        rim_f[...] = rim_f[...] + z_recv[t, 0]
        below = z_recv[t, 1]
        for c in range(comps):
            for i in range(nx):
                at = c * nx + i
                big_f[c, i] = big_f[c, i] + jnp.where(lanes == 0, roll(below, -at, 1), 0.0)

    def contact(t, phase):
        cut = npair // 3 // unroll * unroll
        held = []

        def first():
            if phase > 0:
                wait_all(pos_copies(phase))
            held.append(build_slots(t, phase))
            pair_range(t, 0, cut)

        def middle():
            pair_range(t, cut, npair)
            finish_pairs(t, held[0])

        return [first, middle, lambda: scatter(t)]

    wait_all(pos_copies(0))
    for part in contact(0, 0):
        part()

    for t in range(steps):
        if t == 0:
            big_f[...] = load_f[...]
            rim_f[...] = load_r[...]
        else:
            if t + 1 < steps:
                gather(t)
                for c in pos_copies(t):
                    c.start()
            internal(t)
        for c in range(3):
            big_f[c, 0:cx] = big_f[c, 0:cx] + touch[c]
        halo(t, contact(t + 1, t) if t + 1 < steps else [lambda: None] * 3)
        if t == 0:
            mass = big_f[3]
            minv[...] = jnp.where(mass > 0.0, 1.0 / mass, 0.0)
            held = jnp.where((lanes >= 3 * nx) & (lanes < 4 * nx), rim_f[...], 0.0)
            spread = roll(held, -3 * nx, 1) + roll(held, -2 * nx, 1) + roll(held, -nx, 1)
            minv_r[...] = jnp.where(spread > 0.0, 1.0 / spread, 0.0)
            for c in range(3):
                vel[c] = TIME_STEP * (big_f[c] * minv[...])
            vel_r[...] = TIME_STEP * (rim_f[...] * minv_r[...])
            disp[...] = TIME_STEP * vel[...]
            disp_r[...] = TIME_STEP * vel_r[...]
        else:
            for c in range(3):
                vel[c] = vel[c] + TIME_STEP * (big_f[c] * minv[...])
            vel_r[...] = vel_r[...] + TIME_STEP * (rim_f[...] * minv_r[...])
            disp[...] = disp[...] + TIME_STEP * vel[...]
            disp_r[...] = disp_r[...] + TIME_STEP * vel_r[...]

    rim_value = vel_r[...]
    for c in range(3):
        mean, _, _ = corners(vel, rim_value, c)
        mean = 0.125 * (mean[1:] + mean[:-1])
        for i in range(cx):
            vout_ref[c, :, i, :] = mean[i, 0:cy, :]
    s = stress_of(mod[steps - 1])
    for c in range(6):
        for i in range(cx):
            sout_ref[c, :, i, :] = s[c][i, 0:cy, :]


def per_device(stiffness, density, load, alive, surf_coords, surf_nodes, routes, pairs):
    cx, cy, cz = stiffness.shape
    steps = alive.shape[0]
    sb = surf_coords.shape[0]
    npair = pairs.shape[2]
    count_x, count_y, nz = (lax.axis_size(a) for a in ("gx", "gy", "gz"))
    cap = max(sb // 4, sb // nz)
    nx = cx + 1
    pairt = jnp.transpose(pairs[:, 0], (0, 2, 1))
    sizes = (count_x, count_y, cx, cy, cz, sb, npair, steps, nz, cap)
    vm = lambda *shape: pltpu.VMEM(shape, F32)
    dma = lambda *shape: pltpu.SemaphoreType.DMA(shape)
    column = max(nz - 1, 1)
    scratch = [
        vm(steps + 4, cx, 16, cz), vm(4, nx, 16, cz), vm(16, cz), vm(4, nx, 16, cz), vm(16, cz),
        vm(3, nx, 16, cz), vm(16, cz), vm(3, nx, 16, cz), vm(16, cz), vm(nx, 16, cz), vm(16, cz),
        pltpu.VMEM((nz, 8, 128), jnp.int32), vm(steps - 1, nz, sb, 384), vm(3, 128, 128), vm(nz * cap, 3, 128, 128),
        vm(3, npair, 128), vm(steps, nz, 8, 384), vm(steps, nz, 8, 384), vm(steps, sb, 128), vm(nz, 8, 128),
        pltpu.VMEM((sb, 2 * cx * 16, 128), BF16), vm(sb, cz, 128), pltpu.VMEM((sb, cz, 128), BF16),
        vm(3, cx, 16, cz), pltpu.VMEM((2 * sb * 128, cx * 16), BF16),
        pltpu.VMEM((2 * sb, 3 * cz, 128), BF16),
        vm(steps, 2, 5, 16, cz), vm(steps, 2, 5, 16, cz), vm(steps, 2, 40, cz), vm(steps, 2, 40, cz),
        vm(steps, 2, 16, cz), vm(steps, 2, 16, cz),
        dma(column), dma(column), dma(steps - 1, column), dma(steps - 1, column), dma(steps, column), dma(steps, column),
        dma(steps, 2), dma(steps, 2), dma(steps, 2), dma(steps, 2), dma(steps, 2), dma(steps, 2),
    ]
    vmem = pl.BlockSpec(memory_space=pltpu.VMEM)
    vel, stress = pl.pallas_call(
        functools.partial(body, sizes),
        out_shape=(jax.ShapeDtypeStruct((3, cy, cx, cz), F32), jax.ShapeDtypeStruct((6, cy, cx, cz), F32)),
        in_specs=[vmem] * 8 + [pl.BlockSpec(memory_space=pltpu.SMEM)],
        out_specs=(vmem, vmem),
        scratch_shapes=scratch,
        compiler_params=pltpu.CompilerParams(collective_id=0, has_side_effects=True, vmem_limit_bytes=56 * 1024 * 1024),
    )(jnp.swapaxes(stiffness, 0, 1), jnp.swapaxes(density, 0, 1), jnp.swapaxes(load, 1, 2), jnp.swapaxes(alive, 1, 2),
      jnp.swapaxes(surf_coords, 0, 1), surf_nodes, routes, pairt, pairt)
    return jnp.swapaxes(vel, 1, 2), jnp.swapaxes(stress, 1, 2)


def solution(mesh):
    return jax.shard_map(
        per_device,
        mesh=mesh,
        in_specs=(
            P("gx", "gy", "gz"),
            P("gx", "gy", "gz"),
            P(None, "gx", "gy", "gz"),
            P(None, "gx", "gy", "gz"),
            P(("gx", "gy", "gz"), None, None),
            P(("gx", "gy", "gz"), None),
            P(None, ("gx", "gy", "gz")),
            P(None, ("gx", "gy", "gz"), None, None),
        ),
        out_specs=(P(None, "gx", "gy", "gz"), P(None, "gx", "gy", "gz")),
        check_vma=False,
    )
```

```python
import functools
import math

import jax
import jax.numpy as jnp
from jax import lax
from jax.experimental import pallas as pl
from jax.experimental.pallas import tpu as pltpu
from jax.sharding import PartitionSpec as P

REPULSION = 1.0
KERNEL_SCALE = 0.08
TIME_STEP = 0.2
HIGHEST = lax.Precision.HIGHEST
MESH = pl.DeviceIdType.MESH
F32 = jnp.float32
BF16 = jnp.bfloat16
STRETCH = math.sqrt(math.log2(math.e) / KERNEL_SCALE)


def iota(shape, dim):
    return lax.broadcasted_iota(jnp.int32, shape, dim)


def hdot(a, b):
    return jnp.dot(a, b, preferred_element_type=F32, precision=HIGHEST)


def split2(x):
    high = x.astype(BF16)
    return high, (x - high.astype(F32)).astype(BF16)


def sum_x(q):
    return jnp.concatenate([q[:1], q[:-1] + q[1:], q[-1:]], axis=0)


def diff_x(q):
    return jnp.concatenate([-q[:1], q[:-1] - q[1:], q[-1:]], axis=0)


def body(sizes, stiff_hbm, dens_hbm, load_hbm, alive_hbm, coords_ref, nodes_ref, routes_ref, pairt_ref, pair_ref,
         vout_ref, sout_ref, *scratch):
    (stiff_ref, dens_ref, load_ref, alive_ref, in_sem, mod, big_f, rim_f, load_f, load_r, vel, vel_r, disp, disp_r, minv, minv_r, route_all, pos_all, slots, second,
     partial, send_f, ret, back_pick, rank_in, gather_w, lane_pick, lane_pick_h, touch, scatter_w, scatter_l,
     x_send, x_recv, y_send, y_recv, z_send, z_recv,
     route_ss, route_rs, pos_ss, pos_rs, ret_ss, ret_rs, x_ss, x_rs, y_ss, y_rs, z_ss, z_rs) = scratch
    count_x, count_y, cx, cy, cz, sb, npair, steps, nz, cap = sizes
    nx = cx + 1
    rows = 16
    ix, iy, iz = lax.axis_index("gx"), lax.axis_index("gy"), lax.axis_index("gz")
    lanes = iota((rows, cz), 1)
    lane3 = iota((1, 1, cz), 2)

    def roll(v, shift, axis):
        return pltpu.roll(v, shift % v.shape[axis], axis)

    inputs = [pltpu.make_async_copy(a, b, in_sem.at[k]) for k, (a, b) in enumerate((
        (stiff_hbm, stiff_ref), (alive_hbm, alive_ref), (load_hbm, load_ref), (dens_hbm, dens_ref)))]
    for c in inputs:
        c.start()

    for ref in (x_send, x_recv, y_send, y_recv, z_send, z_recv, mod, slots, send_f):
        ref[...] = jnp.zeros(ref.shape, ref.dtype)

    sides = (("gx", ix, count_x), ("gy", iy, count_y), ("gz", iz, nz))
    barrier = pltpu.get_barrier_semaphore()
    expect = jnp.int32(nz - 1)
    for name, at, count in sides[:2]:
        @pl.when(at > 0)
        def _():
            pl.semaphore_signal(barrier, inc=1, device_id={name: at - 1}, device_id_type=MESH)

        @pl.when(at < count - 1)
        def _():
            pl.semaphore_signal(barrier, inc=1, device_id={name: at + 1}, device_id_type=MESH)
        expect = expect + jnp.where(at > 0, 1, 0) + jnp.where(at < count - 1, 1, 0)
    for other in range(1, nz):
        pl.semaphore_signal(barrier, inc=1, device_id={"gz": lax.rem(iz + other, nz)}, device_id_type=MESH)
    pl.semaphore_wait(barrier, expect)

    def column(send_ref, recv_ref, ss, rs):
        out = []
        for other in range(1, nz):
            to = lax.rem(iz + other, nz)
            out.append(pltpu.make_async_remote_copy(
                src_ref=send_ref(to), dst_ref=recv_ref, send_sem=ss.at[other - 1], recv_sem=rs.at[other - 1],
                device_id={"gz": to}, device_id_type=MESH))
        return out

    def pos_copies(phase):
        return column(lambda to: pos_all.at[phase, iz], pos_all.at[phase, iz], pos_ss.at[phase], pos_rs.at[phase])

    def ret_copies(t):
        return column(lambda to: send_f.at[t, to], ret.at[t, iz], ret_ss.at[t], ret_rs.at[t])

    route_copies = column(lambda to: route_all.at[iz], route_all.at[iz], route_ss, route_rs)

    route_all[iz] = jnp.full((8, 128), -1, jnp.int32)
    route_all[iz, 0:steps, 0:sb] = routes_ref[...]
    for x in range(3):
        pos_all[0, iz, :, x * 128:(x + 1) * 128] = coords_ref[x]
    for c in route_copies + pos_copies(0):
        c.start()

    for c in inputs:
        c.wait()
    for t in range(steps):
        for i in range(cx):
            mod[t, i, 0:cy, :] = stiff_ref[:, i, :] * alive_ref[t, :, i, :].astype(F32)
    for c in range(4):
        for i in range(cx):
            mod[steps + c, i, 0:cy, :] = 0.125 * (load_ref[c, :, i, :] if c < 3 else dens_ref[:, i, :])
    rim = jnp.zeros((rows, cz), F32)
    for c in range(4):
        q = sum_x(mod[steps + c])
        q = q + roll(q, 1, 1)
        r = roll(q, 1, 2)
        load_f[c] = q + jnp.where(lane3 > 0, r, 0.0)
        for i in range(nx):
            at = c * nx + i
            rim = rim + jnp.where(lanes == at, roll(r[i], at, 1), 0.0)
    load_r[...] = rim

    ids = nodes_ref[...]
    row = lax.shift_right_logical(ids, jnp.full(ids.shape, cz.bit_length() - 1, jnp.int32))
    lane = ids & (cz - 1)
    wide = row
    for m in range(1, cx):
        wide = wide + jnp.where(row >= cy * m, rows - cy, 0)
    depth = cx * rows
    wide_pad = jnp.concatenate([wide.astype(F32), jnp.zeros((128 - sb, 128), F32)], axis=0)
    wide_t = jnp.transpose(wide_pad)
    for s in range(sb):
        hot = (iota((depth, 128), 0) == wide[s:s + 1, :]).astype(F32).astype(BF16)
        gather_w[s, 0:depth, :] = hot
        gather_w[s, depth:2 * depth, :] = hot
        pick = (iota((cz, 128), 0) == lane[s:s + 1, :]).astype(F32)
        lane_pick[s] = pick
        lane_pick_h[s] = pick.astype(BF16)
        col = jnp.broadcast_to(wide_t[:, s:s + 1], (128, depth))
        hot = (iota((128, depth), 1).astype(F32) == col).astype(F32).astype(BF16)
        scatter_w[s * 256:s * 256 + 128, :] = hot
        scatter_w[s * 256 + 128:s * 256 + 256, :] = hot

    def wait_all(copies):
        for c in copies:
            c.wait()

    wait_all(route_copies)
    upper = (iota((128, 128), 0) <= iota((128, 128), 1)).astype(F32)
    own = route_all[iz]
    for b in range(nz):
        hits = (route_all[b] == iz).astype(F32)
        rank_in[b] = jnp.where(hits > 0, jnp.dot(hits, upper, preferred_element_type=F32), 0.0)
    slot8 = nz * 8
    picks = []
    for b in range(nz):
        hits = (own == b).astype(F32)
        picks.append(jnp.where(hits > 0, jnp.dot(hits, upper, preferred_element_type=F32), 0.0))
    ranks8 = (iota((8, 128), 0) + 1).astype(F32)
    live8 = iota((8, 128), 0) < cap
    for t in range(steps):
        parts = [jnp.where((picks[b][t:t + 1, :] == ranks8) & live8, 1.0, 0.0) for b in range(nz)]
        table = jnp.concatenate(parts + [jnp.zeros((128 - slot8, 128), F32)], axis=0)
        back_pick[t] = jnp.transpose(table)[0:sb, :]

    def gather(phase):
        highs, lows = [], []
        for c in range(3):
            flat = jnp.transpose(disp[c, 0:cx].reshape(depth, cz))
            high, low = split2(flat)
            highs.append(high)
            lows.append(low)
        left = jnp.concatenate([jnp.concatenate(highs, axis=0), jnp.concatenate(lows, axis=0)], axis=1)
        for s in range(0, sb, 2):
            got = jnp.dot(left, jnp.concatenate([gather_w[s], gather_w[s + 1]], axis=1), preferred_element_type=F32)
            for h in range(2):
                for c in range(3):
                    part = got[c * cz:(c + 1) * cz, h * 128:(h + 1) * 128] * lane_pick[s + h]
                    pos_all[phase, iz, s + h:s + h + 1, c * 128:(c + 1) * 128] = (
                        jnp.sum(part, axis=0, keepdims=True) + coords_ref[c, s + h:s + h + 1, :])

    def build_slots(t, phase):
        live = []
        for b in range(nz):
            hot = jnp.where(rank_in[b, t:t + 1, :] == ranks8[0:cap], 1.0, 0.0)
            live.append(jnp.sum(hot, axis=1, keepdims=True))
            got = STRETCH * hdot(hot[:, 0:sb], pos_all[phase, b])
            for x in range(3):
                slots[x, b * cap:(b + 1) * cap, :] = got[:, x * 128:(x + 1) * 128]
        for x in range(3):
            flipped = jnp.transpose(slots[x])
            for k in range(nz * cap):
                second[k, x] = jnp.broadcast_to(flipped[:, k:k + 1], (128, 128))
        return live

    unroll = 4

    def pair_range(t, start, stop):
        def some(at, carry):
            for u in range(unroll):
                one(start + at * unroll + u)
            return carry

        def one(q):
            p = pair_ref[t, 0, q]
            r = pair_ref[t, 1, q]
            xi = [jnp.broadcast_to(slots[x, pl.ds(p, 1), :], (8, 128)) for x in range(3)]
            acc = [jnp.zeros((8, 128), F32)] * 3
            for j in range(16):
                d = [xi[x] - second[r, x, j * 8:(j + 1) * 8, :] for x in range(3)]
                w = jnp.exp2(-(d[0] * d[0] + d[1] * d[1] + d[2] * d[2]))
                acc = [acc[x] + d[x] * w for x in range(3)]
            for x in range(3):
                partial[x, pl.ds(q, 1), :] = jnp.sum(acc[x], axis=0, keepdims=True)
        lax.fori_loop(0, (stop - start) // unroll, some, 0)

    def finish_pairs(t, live):
        first = pairt_ref[t, 0:1, :]
        other = pairt_ref[t, 1:2, :]
        live_p = jnp.zeros((1, npair), F32)
        live_r = jnp.zeros((1, npair), F32)
        for b in range(nz):
            slot = iota((cap, npair), 0) + b * cap
            live_p = live_p + jnp.sum(jnp.where(first == slot, live[b], 0.0), axis=0, keepdims=True)
            live_r = live_r + jnp.sum(jnp.where(other == slot, live[b], 0.0), axis=0, keepdims=True)
        weight = live_p * live_r * (REPULSION / STRETCH)
        for b in range(nz):
            hot = jnp.where(first == iota((cap, npair), 0) + b * cap, weight, 0.0)
            for x in range(3):
                send_f[t, b, 0:cap, x * 128:(x + 1) * 128] = hdot(hot, partial[x])
        for c in ret_copies(t):
            c.start()
        ret[t, iz] = send_f[t, iz]

    def scatter(t):
        wait_all(ret_copies(t))
        force = hdot(back_pick[t, :, 0:slot8], ret[t].reshape(slot8, 384))
        for c in range(3):
            for s in range(sb):
                line = jnp.broadcast_to(force[s:s + 1, c * 128:(c + 1) * 128], (16, 128))
                for h, half in enumerate(split2(line)):
                    spread = lane_pick_h[s].reshape(cz // 16, 16, 128) * half[None]
                    scatter_l[2 * s + h, c * cz:(c + 1) * cz, :] = spread.reshape(cz, 128)
        left = jnp.concatenate([scatter_l[k] for k in range(2 * sb)], axis=1)
        total = jnp.dot(left, scatter_w[...], preferred_element_type=F32)
        for c in range(3):
            grid = jnp.transpose(total[c * cz:(c + 1) * cz, :]).reshape(cx, rows, cz)
            touch[c] = grid

    def corners(field, rim_value, c):
        u = field[c]
        edge = jnp.stack([roll(rim_value, -(c * nx + i), 1) for i in range(nx)])
        above = roll(jnp.where(lane3 == 0, edge, u), -1, 2)
        both = u + above
        step = above - u
        shifted = roll(both, -1, 1)
        return both + shifted, shifted - both, step + roll(step, -1, 1)

    def stress_of(modulus):
        grads = []
        rim_value = disp_r[...]
        for c in range(3):
            mean, along_y, along_z = corners(disp, rim_value, c)
            grads.append((0.25 * (mean[1:] - mean[:-1]), 0.25 * (along_y[1:] + along_y[:-1]),
                          0.25 * (along_z[1:] + along_z[:-1])))
        trace = grads[0][0] + grads[1][1] + grads[2][2]
        return (modulus * (2.0 * grads[0][0] + trace), modulus * (2.0 * grads[1][1] + trace),
                modulus * (2.0 * grads[2][2] + trace), modulus * (grads[0][1] + grads[1][0]),
                modulus * (grads[1][2] + grads[2][1]), modulus * (grads[0][2] + grads[2][0]))

    def internal(t):
        s = stress_of(mod[t])
        table = ((s[0], s[3], s[5]), (s[3], s[1], s[4]), (s[5], s[4], s[2]))
        rim = load_r[...]
        for c in range(3):
            a0 = -0.25 * diff_x(table[c][0])
            ay = -0.25 * sum_x(table[c][1])
            az = -0.25 * sum_x(table[c][2])
            a = (a0 - ay) + roll(a0 + ay, 1, 1)
            b = az + roll(az, 1, 1)
            r = roll(a + b, 1, 2)
            big_f[c] = load_f[c] + (a - b) + jnp.where(lane3 > 0, r, 0.0)
            for i in range(nx):
                at = c * nx + i
                rim = rim + jnp.where(lanes == at, roll(r[i], at, 1), 0.0)
        rim_f[...] = rim

    def axis_copies(side, send, recv, ss, rs, t, used):
        name, at, count = side
        out = []
        for way, to, sends, gets in ((0, at - 1, at > 0, at < count - 1), (1, at + 1, at < count - 1, at > 0)):
            out.append((pltpu.make_async_remote_copy(
                src_ref=send.at[t, way, 0:used], dst_ref=recv.at[t, way, 0:used], send_sem=ss.at[t, way],
                recv_sem=rs.at[t, way], device_id={name: to}, device_id_type=MESH), sends, gets))
        return out

    def start(copies):
        for copy, sends, _ in copies:
            @pl.when(sends)
            def _():
                copy.start()

    def finish(copies):
        for copy, sends, gets in copies:
            @pl.when(sends)
            def _():
                copy.wait_send()

            @pl.when(gets)
            def _():
                copy.wait_recv()

    def halo(t, fillers):
        comps = 4 if t == 0 else 3
        low_lane = functools.reduce(jnp.logical_or, [lanes == c * nx for c in range(4)])
        high_lane = functools.reduce(jnp.logical_or, [lanes == c * nx + cx for c in range(4)])
        for way, plane in ((0, 0), (1, cx)):
            x_send[t, way, 0] = rim_f[...]
            for c in range(comps):
                x_send[t, way, 1 + c] = big_f[c, plane]
        copies = axis_copies(sides[0], x_send, x_recv, x_ss, x_rs, t, comps + 1)
        start(copies)
        fillers[0]()
        finish(copies)
        for c in range(comps):
            big_f[c, 0] = big_f[c, 0] + x_recv[t, 1, 1 + c]
            big_f[c, cx] = big_f[c, cx] + x_recv[t, 0, 1 + c]
        rim_f[...] = (rim_f[...] + jnp.where(low_lane, roll(x_recv[t, 1, 0], -cx, 1), 0.0)
                      + jnp.where(high_lane, roll(x_recv[t, 0, 0], cx, 1), 0.0))

        used = -(-(1 + comps * nx) // 8) * 8
        for way, line in ((0, 0), (1, cy)):
            y_send[t, way, 0:1] = rim_f[line:line + 1]
            for c in range(comps):
                for i in range(nx):
                    at = 1 + c * nx + i
                    y_send[t, way, at:at + 1] = big_f[c, i, line:line + 1]
        copies = axis_copies(sides[1], y_send, y_recv, y_ss, y_rs, t, used)
        start(copies)
        fillers[1]()
        finish(copies)
        for way, line in ((1, 0), (0, cy)):
            rim_f[line:line + 1] = rim_f[line:line + 1] + y_recv[t, way, 0:1]
            for c in range(comps):
                for i in range(nx):
                    at = 1 + c * nx + i
                    big_f[c, i, line:line + 1] = big_f[c, i, line:line + 1] + y_recv[t, way, at:at + 1]

        packed = jnp.zeros((rows, cz), F32)
        for c in range(comps):
            for i in range(nx):
                at = c * nx + i
                packed = jnp.where(lanes == at, roll(big_f[c, i], at, 1), packed)
        z_send[t, 0] = packed
        z_send[t, 1] = rim_f[...]
        copies = axis_copies(sides[2], z_send, z_recv, z_ss, z_rs, t, rows)
        start(copies)
        fillers[2]()
        finish(copies)
        rim_f[...] = rim_f[...] + z_recv[t, 0]
        below = z_recv[t, 1]
        for c in range(comps):
            for i in range(nx):
                at = c * nx + i
                big_f[c, i] = big_f[c, i] + jnp.where(lanes == 0, roll(below, -at, 1), 0.0)

    def contact(t, phase):
        cut = npair // (3 if phase > 0 else 2) // unroll * unroll
        held = []

        def first():
            if phase > 0:
                wait_all(pos_copies(phase))
                held.append(build_slots(t, phase))
            else:
                held.append(early)
            pair_range(t, 0, cut)

        def middle():
            pair_range(t, cut, npair)
            finish_pairs(t, held[0])

        return [first, middle, lambda: scatter(t)]

    wait_all(pos_copies(0))
    live = build_slots(0, 0)
    pair_range(0, 0, npair)
    finish_pairs(0, live)
    early = build_slots(1, 0)
    scatter(0)

    for t in range(steps):
        if t == 0:
            big_f[...] = load_f[...]
            rim_f[...] = load_r[...]
        else:
            if t + 1 < steps:
                gather(t)
                for c in pos_copies(t):
                    c.start()
            internal(t)
        for c in range(3):
            big_f[c, 0:cx] = big_f[c, 0:cx] + touch[c]
        halo(t, contact(t + 1, t) if t + 1 < steps else [lambda: None] * 3)
        if t == 0:
            mass = big_f[3]
            minv[...] = jnp.where(mass > 0.0, 1.0 / mass, 0.0)
            held = jnp.where((lanes >= 3 * nx) & (lanes < 4 * nx), rim_f[...], 0.0)
            spread = roll(held, -3 * nx, 1) + roll(held, -2 * nx, 1) + roll(held, -nx, 1)
            minv_r[...] = jnp.where(spread > 0.0, 1.0 / spread, 0.0)
            for c in range(3):
                vel[c] = TIME_STEP * (big_f[c] * minv[...])
            vel_r[...] = TIME_STEP * (rim_f[...] * minv_r[...])
            disp[...] = TIME_STEP * vel[...]
            disp_r[...] = TIME_STEP * vel_r[...]
        else:
            for c in range(3):
                vel[c] = vel[c] + TIME_STEP * (big_f[c] * minv[...])
            vel_r[...] = vel_r[...] + TIME_STEP * (rim_f[...] * minv_r[...])
            disp[...] = disp[...] + TIME_STEP * vel[...]
            disp_r[...] = disp_r[...] + TIME_STEP * vel_r[...]

    rim_value = vel_r[...]
    for c in range(3):
        mean, _, _ = corners(vel, rim_value, c)
        mean = 0.125 * (mean[1:] + mean[:-1])
        for i in range(cx):
            vout_ref[c, :, i, :] = mean[i, 0:cy, :]
    s = stress_of(mod[steps - 1])
    for c in range(6):
        for i in range(cx):
            sout_ref[c, :, i, :] = s[c][i, 0:cy, :]


def per_device(stiffness, density, load, alive, surf_coords, surf_nodes, routes, pairs):
    cx, cy, cz = stiffness.shape
    steps = alive.shape[0]
    sb = surf_coords.shape[0]
    npair = pairs.shape[2]
    count_x, count_y, nz = (lax.axis_size(a) for a in ("gx", "gy", "gz"))
    cap = max(sb // 4, sb // nz)
    nx = cx + 1
    pairt = jnp.transpose(pairs[:, 0], (0, 2, 1))
    sizes = (count_x, count_y, cx, cy, cz, sb, npair, steps, nz, cap)
    vm = lambda *shape: pltpu.VMEM(shape, F32)
    dma = lambda *shape: pltpu.SemaphoreType.DMA(shape)
    column = max(nz - 1, 1)
    scratch = [
        vm(cy, cx, cz), vm(cy, cx, cz), vm(3, cy, cx, cz), pltpu.VMEM((steps, cy, cx, cz), jnp.int32), dma(4),
        vm(steps + 4, cx, 16, cz), vm(4, nx, 16, cz), vm(16, cz), vm(4, nx, 16, cz), vm(16, cz),
        vm(3, nx, 16, cz), vm(16, cz), vm(3, nx, 16, cz), vm(16, cz), vm(nx, 16, cz), vm(16, cz),
        pltpu.VMEM((nz, 8, 128), jnp.int32), vm(steps - 1, nz, sb, 384), vm(3, 128, 128), vm(nz * cap, 3, 128, 128),
        vm(3, npair, 128), vm(steps, nz, 8, 384), vm(steps, nz, 8, 384), vm(steps, sb, 128), vm(nz, 8, 128),
        pltpu.VMEM((sb, 2 * cx * 16, 128), BF16), vm(sb, cz, 128), pltpu.VMEM((sb, cz, 128), BF16),
        vm(3, cx, 16, cz), pltpu.VMEM((2 * sb * 128, cx * 16), BF16),
        pltpu.VMEM((2 * sb, 3 * cz, 128), BF16),
        vm(steps, 2, 5, 16, cz), vm(steps, 2, 5, 16, cz), vm(steps, 2, 40, cz), vm(steps, 2, 40, cz),
        vm(steps, 2, 16, cz), vm(steps, 2, 16, cz),
        dma(column), dma(column), dma(steps - 1, column), dma(steps - 1, column), dma(steps, column), dma(steps, column),
        dma(steps, 2), dma(steps, 2), dma(steps, 2), dma(steps, 2), dma(steps, 2), dma(steps, 2),
    ]
    vmem = pl.BlockSpec(memory_space=pltpu.VMEM)
    vel, stress = pl.pallas_call(
        functools.partial(body, sizes),
        out_shape=(jax.ShapeDtypeStruct((3, cy, cx, cz), F32), jax.ShapeDtypeStruct((6, cy, cx, cz), F32)),
        in_specs=[pl.BlockSpec(memory_space=pltpu.MemorySpace.HBM)] * 4 + [vmem] * 4 + [pl.BlockSpec(memory_space=pltpu.SMEM)],
        out_specs=(vmem, vmem),
        scratch_shapes=scratch,
        compiler_params=pltpu.CompilerParams(collective_id=0, has_side_effects=True, vmem_limit_bytes=56 * 1024 * 1024),
    )(jnp.swapaxes(stiffness, 0, 1), jnp.swapaxes(density, 0, 1), jnp.swapaxes(load, 1, 2), jnp.swapaxes(alive, 1, 2),
      jnp.swapaxes(surf_coords, 0, 1), surf_nodes, routes, pairt, pairt)
    return jnp.swapaxes(vel, 1, 2), jnp.swapaxes(stress, 1, 2)


def solution(mesh):
    return jax.shard_map(
        per_device,
        mesh=mesh,
        in_specs=(
            P("gx", "gy", "gz"),
            P("gx", "gy", "gz"),
            P(None, "gx", "gy", "gz"),
            P(None, "gx", "gy", "gz"),
            P(("gx", "gy", "gz"), None, None),
            P(("gx", "gy", "gz"), None),
            P(None, ("gx", "gy", "gz")),
            P(None, ("gx", "gy", "gz"), None, None),
        ),
        out_specs=(P(None, "gx", "gy", "gz"), P(None, "gx", "gy", "gz")),
        check_vma=False,
    )
```
